32 devices in a mesh: rep: 2 (over y), pair: 8 (over z, x), samp: 2 (over core).
Axes of the slice: x: 2, y: 2, z: 4, core: 2. Of those that a mesh axis runs over, the one named last changes fastest.
Arguments:
- dosage: bfloat16 [128, 4096], P(('rep', 'pair', 'samp')), parts along dimension 0, may hold values from 0 to 2
- phenotype: bfloat16 [2, 128], P(None, ('rep', 'pair', 'samp')), parts along dimension 1, may hold values from -6 to 6
- perms: int32 [2, 64], replicated, may hold values from 0 to 63, each once within a row
- pairs: int32 [8, 2], replicated, may hold values from 0 to 7
Outputs:
- stat: bfloat16 [16, 4, 512, 512], P(('rep', 'pair'), None, None, 'samp'), parts along dimension 0
The draws below stay inside these ranges and needn't reach their ends.
There are 2 independent parts, one for each index of `rep`. The reference program is written for one: setup_inputs(seed, part) draws one part's arguments, and reference() takes and returns one part's arrays. A program takes and returns all parts, laid end to end along the dimension named above; an argument that names none is the same for every part. Nothing has to cross between parts.
Inputs may be any that keep to these rules, and one draw needn't show every extreme that they name: `perms`: each row is a permutation of the samples. `pairs`: panel ids; a panel may appear in many blocks.
All inputs are finite; a program needn't handle non-finite values.
Results may differ from the reference program's by a relative error of at most 0.02.
Values may be sent and summed in bfloat16 or wider, within the bound.
A program may use at most 64 MiB of HBM per device.

```python
import math
import jax
import jax.numpy as jnp
import numpy as np
from jax import lax

PANEL = 512
GENES = 2
PERMS = 2
NB = 8
NPANEL = 8
SNPS = 4096
SAMPLES = 64


def plant(drawn, rng, least, largest):
    dims = drawn.shape
    spot = [jax.random.randint(jax.random.fold_in(rng, axis), (), 0, dims[axis]) for axis in range(len(dims))]
    drawn = drawn.at[tuple(spot)].set(least)
    longest = dims.index(max(dims))
    spot[longest] = (spot[longest] + 1) % dims[longest]
    return drawn.at[tuple(spot)].set(largest)


def shard_levels(own_key, extent, shards, low, largest):
    level = 1.0
    for position, parts in shards:
        heights = jax.random.uniform(jax.random.fold_in(jax.random.fold_in(own_key, 6), position), (parts,), jnp.float32, low / len(shards), largest / len(shards))
        level = level * jnp.repeat(jnp.exp(heights), extent[position] // parts).reshape((-1,) + (1,) * (len(extent) - 1 - position))
    return level


def rank_bounds(number_of, slope):
    loads = [(1 << 20) // math.isqrt(standing ** slope) + 1 for standing in range(1, number_of + 1)]
    width = 1 + sum(loads) // (1 << 30)
    return np.cumsum(np.array([max(1, weight // width) for weight in loads]))


def ranked_ids(stream_key, shape, count, lean):
    listing = rank_bounds(count, lean)
    lot = jax.random.randint(jax.random.fold_in(stream_key, 1), shape, 0, int(listing[count - 1]))
    grade = jnp.searchsorted(jnp.asarray(listing, jnp.int32), lot, side="right")
    return jax.random.permutation(jax.random.fold_in(stream_key, 2), count)[grade].astype(jnp.int32)


def normal_values(rng, extent, scale, bound, cuts=(), dtype=jnp.bfloat16):
    values = jax.random.normal(rng, extent, jnp.float32) * scale
    if len(cuts) > 0:
        values = shard_levels(rng, extent, cuts, -0.22, 0.18) * values
    return jnp.clip(values, min=-bound, max=bound).astype(dtype)


def setup_inputs(seed: int = 0, part: int = 0) -> dict:
    streams_of = jax.random.split(jax.random.key(seed), 5)
    own_keys = jax.random.split(jax.random.fold_in(streams_of[4], part), 5)
    return {
        "dosage": jnp.clip(2.0 * jax.random.uniform(own_keys[0], (SAMPLES, SNPS), jnp.float32) ** shard_levels(own_keys[0], (SAMPLES, SNPS), ((0, 16),), -0.2, 0.2), 0.0, 2.0).astype(jnp.bfloat16),
        "phenotype": normal_values(own_keys[1], (GENES, SAMPLES), 1.0, 6.0, ((1, 16),)),
        "perms": jax.vmap(lambda own: jax.random.permutation(own, SAMPLES))(jax.random.split(streams_of[2], PERMS)).reshape((PERMS, SAMPLES)).astype(jnp.int32),
        "pairs": plant(ranked_ids(streams_of[3], (NB, 2), NPANEL, 2), jax.random.fold_in(streams_of[3], 3), 0, NPANEL - 1).astype(jnp.int32),
    }


def reference(dosage, phenotype, perms, pairs):
    total = dosage.shape[0]
    count = jnp.float32(total)
    pheno = phenotype.astype(jnp.float32)
    yperm = pheno[:, perms].reshape(GENES * PERMS, total)
    grouped = dosage.reshape(total, NPANEL, PANEL)

    def one_block(pair):
        geno_a = lax.dynamic_index_in_dim(grouped, pair[0], 1, keepdims=False).astype(jnp.float32)
        geno_b = lax.dynamic_index_in_dim(grouped, pair[1], 1, keepdims=False).astype(jnp.float32)
        scaled = (yperm[:, :, None] * geno_a[None]).astype(jnp.bfloat16).astype(jnp.float32)
        prod = jnp.einsum('ksi,sj->kij', scaled, geno_b, precision=lax.Precision.HIGHEST)
        ya = lax.optimization_barrier(jnp.sum(scaled, axis=1))
        yb = jnp.einsum('ks,sj->kj', yperm, geno_b, precision=lax.Precision.HIGHEST)
        marg_a = lax.optimization_barrier(jnp.sum(geno_a, axis=0))
        marg_b = lax.optimization_barrier(jnp.sum(geno_b, axis=0))
        ysum = lax.optimization_barrier(jnp.sum(yperm, axis=1))
        value = prod - ya[:, :, None] * marg_b[None, None, :] / count
        value = value - marg_a[None, :, None] * yb[:, None, :] / count
        value = value + marg_a[None, :, None] * marg_b[None, None, :] * ysum[:, None, None] / (count * count)
        return (value / jnp.sqrt(count)).astype(jnp.bfloat16)
    return lax.map(one_block, pairs)
```

```python
import functools

import jax
import jax.numpy as jnp
from jax import lax
from jax.experimental import pallas as pl
from jax.experimental.pallas import tpu as pltpu
from jax.sharding import PartitionSpec as P

PANEL = 512
LANES = 128


def exchange(n, samp, pairs_ref, dosage_ref, pheno_ref, out_ref, send_buf, send_sem, recv_sem):
    half = PANEL // samp
    me = lax.axis_index("pair") * samp + lax.axis_index("samp")
    s_dev = dosage_ref.shape[0]

    barrier = pltpu.get_barrier_semaphore()

    def greet(d, carry):
        dest = lax.rem(me + d, n)
        pl.semaphore_signal(
            barrier, inc=1, device_id={"pair": dest // samp, "samp": dest % samp},
            device_id_type=pl.DeviceIdType.MESH,
        )
        return carry

    lax.fori_loop(1, n, greet, 0)

    row = lax.broadcasted_iota(jnp.int32, (s_dev, s_dev), 0)
    col = lax.broadcasted_iota(jnp.int32, (s_dev, s_dev), 1)
    lane = lax.broadcasted_iota(jnp.int32, (s_dev, LANES), 1)
    tail = jnp.zeros((s_dev, LANES), jnp.float32)
    for g in range(pheno_ref.shape[0]):
        values = pheno_ref[...].astype(jnp.float32)[g : g + 1, :]
        column = jnp.sum(jnp.where(row == col, values, 0.0), axis=1, keepdims=True)
        tail = jnp.where(lane == g, column, tail)
    tail = tail.astype(jnp.bfloat16)

    panels = dosage_ref.shape[1] // PANEL

    def fill(b, carry):
        first = jnp.full((s_dev, PANEL), pairs_ref[0, b], jnp.int32)
        second = jnp.full((s_dev, PANEL), pairs_ref[1, b], jnp.int32)

        def pick(p, kept):
            at = p * PANEL if isinstance(p, int) else pl.multiple_of(p * PANEL, PANEL)
            panel = dosage_ref[:, pl.ds(at, PANEL)].astype(jnp.float32)
            return jnp.where(first == p, panel, kept[0]), jnp.where(second == p, panel, kept[1])

        kept = (jnp.zeros((s_dev, PANEL), jnp.float32),) * 2
        if panels <= 16:
            for p in range(panels):
                kept = pick(p, kept)
        else:
            kept = lax.fori_loop(0, panels, pick, kept)
        geno_a, geno_b = (x.astype(jnp.bfloat16) for x in kept)
        for c in range(samp):
            send_buf[b * samp + c, :, :PANEL] = geno_a
            send_buf[b * samp + c, :, PANEL : PANEL + half] = geno_b[:, c * half : (c + 1) * half]
            send_buf[b * samp + c, :, PANEL + half :] = tail
        return carry

    lax.fori_loop(0, n // samp, fill, 0)
    pl.semaphore_wait(barrier, n - 1)

    own = pltpu.make_async_copy(send_buf.at[me], out_ref.at[me], recv_sem)
    own.start()

    def send(d, carry):
        dest = lax.rem(me + d, n)
        pltpu.make_async_remote_copy(
            src_ref=send_buf.at[dest],
            dst_ref=out_ref.at[me],
            send_sem=send_sem,
            recv_sem=recv_sem,
            device_id={"pair": dest // samp, "samp": dest % samp},
            device_id_type=pl.DeviceIdType.MESH,
        ).start()
        return carry

    lax.fori_loop(1, n, send, 0)
    pltpu.make_async_copy(out_ref, out_ref, recv_sem).wait()
    rest = send_buf.at[pl.ds(0, n - 1)]
    pltpu.make_async_copy(rest, rest, send_sem).wait()


def statistics(half, perms_ref, recv_ref, out_ref, tiles, sems):
    n, s_dev, _ = recv_ref.shape
    count = n * s_dev
    genes = tiles.shape[0] // perms_ref.shape[0]
    perms_n = perms_ref.shape[0]
    rows = jnp.concatenate([recv_ref[i].astype(jnp.float32) for i in range(n)], axis=0)
    geno_a = rows[:, :PANEL]
    geno_b = rows[:, PANEL : PANEL + half]
    pheno = rows[:, PANEL + half :].T[:8].astype(jnp.bfloat16)

    a_twice = jnp.concatenate([geno_a, geno_a], axis=0).T
    a_low = a_twice.astype(jnp.bfloat16)

    marg_b = jnp.sum(geno_b, axis=0, keepdims=True)
    centred = (geno_b - marg_b * (1.0 / count)) * (1.0 / count**0.5)
    high = centred.astype(jnp.bfloat16)
    low = (centred - high.astype(jnp.float32)).astype(jnp.bfloat16)
    b_split = jnp.concatenate([high, low], axis=0)

    sample = lax.broadcasted_iota(jnp.int32, (count, 2 * count), 0)
    picked = []
    for r in range(perms_n):
        order = perms_ref[r : r + 1, :]
        order = jnp.concatenate([order, order], axis=1)
        hot = jnp.where(sample == order, 1.0, 0.0).astype(jnp.bfloat16)
        picked.append(jnp.dot(pheno, hot, preferred_element_type=jnp.float32))
    slopes = [
        jnp.dot(picked[r].astype(jnp.bfloat16), b_split, preferred_element_type=jnp.float32)
        * (-1.0 / count)
        for r in range(perms_n)
    ]
    copies = []
    for k in range(genes * perms_n):
        g, r = k // perms_n, k % perms_n
        y = picked[r][g : g + 1, :]
        scaled = (a_twice * y).astype(jnp.bfloat16)
        slope = slopes[r][g : g + 1, :]
        slope_high = slope.astype(jnp.bfloat16).astype(jnp.float32)
        slope_low = slope - slope_high
        slope_rows = jnp.concatenate(
            [
                jnp.broadcast_to(slope_high, (count, half)),
                jnp.broadcast_to(slope_low, (count, half)),
            ],
            axis=0,
        ).astype(jnp.bfloat16)
        left = jnp.concatenate([scaled, a_low], axis=1)
        right = jnp.concatenate([b_split, slope_rows], axis=0)
        tiles[k] = jnp.dot(left, right, preferred_element_type=jnp.float32).astype(jnp.bfloat16)
        copy = pltpu.make_async_copy(tiles.at[k], out_ref.at[0, k], sems.at[k])
        copy.start()
        copies.append(copy)
    for copy in copies:
        copy.wait()


def on_device(dosage, phenotype, perms, pairs):
    samp = lax.axis_size("samp")
    n = lax.axis_size("pair") * samp
    half = PANEL // samp
    s_dev = dosage.shape[0]
    width = PANEL + half + LANES
    kinds = phenotype.shape[0] * perms.shape[0]
    vmem = pl.BlockSpec(memory_space=pltpu.VMEM)
    smem = pl.BlockSpec(memory_space=pltpu.SMEM)
    received = pl.pallas_call(
        functools.partial(exchange, n, samp),
        out_shape=jax.ShapeDtypeStruct((n, s_dev, width), jnp.bfloat16),
        in_specs=[smem, vmem, vmem],
        out_specs=vmem,
        scratch_shapes=[
            pltpu.VMEM((n, s_dev, width), jnp.bfloat16),
            pltpu.SemaphoreType.DMA,
            pltpu.SemaphoreType.DMA,
        ],
        compiler_params=pltpu.CompilerParams(collective_id=0, has_side_effects=True),
        name="exchange",
    )(pairs.T, dosage, phenotype)
    return pl.pallas_call(
        functools.partial(statistics, half),
        out_shape=jax.ShapeDtypeStruct((1, kinds, PANEL, half), jnp.bfloat16),
        in_specs=[vmem, vmem],
        out_specs=pl.BlockSpec(memory_space=pl.ANY),
        scratch_shapes=[
            pltpu.VMEM((kinds, PANEL, half), jnp.bfloat16),
            pltpu.SemaphoreType.DMA((kinds,)),
        ],
        name="statistics",
    )(perms, received)


def solution(mesh):
    placed = (P(("rep", "pair", "samp"), None), P(None, ("rep", "pair", "samp")), P(), P())
    return jax.shard_map(
        on_device,
        mesh=mesh,
        in_specs=placed,
        out_specs=P(("rep", "pair"), None, None, "samp"),
        check_vma=False,
    )
```

```python
import functools

import jax
import jax.numpy as jnp
from jax import lax
from jax.experimental import pallas as pl
from jax.experimental.pallas import tpu as pltpu
from jax.sharding import PartitionSpec as P

PANEL = 512
LANES = 128


def partner(me, m, n):
    if n & (n - 1):
        return lax.rem(me + m, n)
    dest, weight = 0, 1
    while weight < n:
        dest = dest + (me // weight + m // weight) % 2 * weight
        weight *= 2
    return dest


def exchange(
    n, samp, pairs_hbm, dosage_hbm, pheno_hbm, out_ref,
    pairs_ref, dosage_ref, pheno_ref, send_buf, in_sems, send_sem, recv_sem,
):
    half = PANEL // samp
    me = lax.axis_index("pair") * samp + lax.axis_index("samp")
    s_dev = dosage_ref.shape[0]

    inputs = [
        pltpu.make_async_copy(dosage_hbm, dosage_ref, in_sems.at[0]),
        pltpu.make_async_copy(pheno_hbm, pheno_ref, in_sems.at[1]),
        pltpu.make_async_copy(pairs_hbm, pairs_ref, in_sems.at[2]),
    ]
    for copy in inputs:
        copy.start()
    barrier = pltpu.get_barrier_semaphore()

    def greet(i, carry):
        dest = partner(me, n - 1 - i, n)
        pl.semaphore_signal(
            barrier, inc=1, device_id={"pair": dest // samp, "samp": dest % samp},
            device_id_type=pl.DeviceIdType.MESH,
        )
        return carry

    lax.fori_loop(0, n - 1, greet, 0, unroll=n <= 16)
    for copy in inputs:
        copy.wait()

    row = lax.broadcasted_iota(jnp.int32, (s_dev, s_dev), 0)
    col = lax.broadcasted_iota(jnp.int32, (s_dev, s_dev), 1)
    lane = lax.broadcasted_iota(jnp.int32, (s_dev, LANES), 1)
    tail = jnp.zeros((s_dev, LANES), jnp.float32)
    for g in range(pheno_ref.shape[0]):
        values = pheno_ref[...].astype(jnp.float32)[g : g + 1, :]
        column = jnp.sum(jnp.where(row == col, values, 0.0), axis=1, keepdims=True)
        tail = jnp.where(lane == g, column, tail)
    tail = tail.astype(jnp.bfloat16)

    panels = dosage_ref.shape[1] // PANEL

    def fill(b, carry):
        first = jnp.full((s_dev, PANEL), pairs_ref[0, b], jnp.int32)
        second = jnp.full((s_dev, PANEL), pairs_ref[1, b], jnp.int32)

        def pick(p, kept):
            at = p * PANEL if isinstance(p, int) else pl.multiple_of(p * PANEL, PANEL)
            panel = dosage_ref[:, pl.ds(at, PANEL)].astype(jnp.float32)
            return jnp.where(first == p, panel, kept[0]), jnp.where(second == p, panel, kept[1])

        kept = (jnp.zeros((s_dev, PANEL), jnp.float32),) * 2
        if panels <= 16:
            for p in range(panels):
                kept = pick(p, kept)
        else:
            kept = lax.fori_loop(0, panels, pick, kept)
        geno_a, geno_b = (x.astype(jnp.bfloat16) for x in kept)
        for c in range(samp):
            send_buf[b * samp + c, :, :PANEL] = geno_a
            send_buf[b * samp + c, :, PANEL : PANEL + half] = geno_b[:, c * half : (c + 1) * half]
            send_buf[b * samp + c, :, PANEL + half :] = tail
        return carry

    lax.fori_loop(0, n // samp, fill, 0)
    pl.semaphore_wait(barrier, n - 1)

    def send(i, carry):
        dest = partner(me, n - 1 - i, n)
        pltpu.make_async_remote_copy(
            src_ref=send_buf.at[dest],
            dst_ref=out_ref.at[me],
            send_sem=send_sem,
            recv_sem=recv_sem,
            device_id={"pair": dest // samp, "samp": dest % samp},
            device_id_type=pl.DeviceIdType.MESH,
        ).start()
        return carry

    lax.fori_loop(0, n - 1, send, 0, unroll=n <= 16)
    pltpu.make_async_copy(send_buf.at[me], out_ref.at[me], recv_sem).start()
    pltpu.make_async_copy(out_ref, out_ref, recv_sem).wait()
    rest = send_buf.at[pl.ds(0, n - 1)]
    pltpu.make_async_copy(rest, rest, send_sem).wait()


def statistics(half, perms_ref, recv_ref, out_ref, tiles, sems):
    n, s_dev, _ = recv_ref.shape
    count = n * s_dev
    genes = tiles.shape[0] // perms_ref.shape[0]
    perms_n = perms_ref.shape[0]
    rows = jnp.concatenate([recv_ref[i].astype(jnp.float32) for i in range(n)], axis=0)
    geno_a = rows[:, :PANEL]
    geno_b = rows[:, PANEL : PANEL + half]
    pheno = rows[:, PANEL + half :].T[:8].astype(jnp.bfloat16)

    a_twice = jnp.concatenate([geno_a, geno_a], axis=0).T
    a_low = a_twice.astype(jnp.bfloat16)

    marg_b = jnp.sum(geno_b, axis=0, keepdims=True)
    centred = (geno_b - marg_b * (1.0 / count)) * (1.0 / count**0.5)
    high = centred.astype(jnp.bfloat16)
    low = (centred - high.astype(jnp.float32)).astype(jnp.bfloat16)
    b_split = jnp.concatenate([high, low], axis=0)

    sample = lax.broadcasted_iota(jnp.int32, (count, 2 * count), 0)
    picked = []
    for r in range(perms_n):
        order = perms_ref[r : r + 1, :]
        order = jnp.concatenate([order, order], axis=1)
        hot = jnp.where(sample == order, 1.0, 0.0).astype(jnp.bfloat16)
        picked.append(jnp.dot(pheno, hot, preferred_element_type=jnp.float32))
    slopes = [
        jnp.dot(picked[r].astype(jnp.bfloat16), b_split, preferred_element_type=jnp.float32)
        * (-1.0 / count)
        for r in range(perms_n)
    ]
    copies = []
    for k in range(genes * perms_n):
        g, r = k // perms_n, k % perms_n
        y = picked[r][g : g + 1, :]
        scaled = (a_twice * y).astype(jnp.bfloat16)
        slope = slopes[r][g : g + 1, :]
        slope_high = slope.astype(jnp.bfloat16).astype(jnp.float32)
        slope_low = slope - slope_high
        slope_rows = jnp.concatenate(
            [
                jnp.broadcast_to(slope_high, (count, half)),
                jnp.broadcast_to(slope_low, (count, half)),
            ],
            axis=0,
        ).astype(jnp.bfloat16)
        left = jnp.concatenate([scaled, a_low], axis=1)
        right = jnp.concatenate([b_split, slope_rows], axis=0)
        tiles[k] = jnp.dot(left, right, preferred_element_type=jnp.float32).astype(jnp.bfloat16)
        copy = pltpu.make_async_copy(tiles.at[k], out_ref.at[0, k], sems.at[k])
        copy.start()
        copies.append(copy)
    for copy in copies:
        copy.wait()


def on_device(dosage, phenotype, perms, pairs):
    samp = lax.axis_size("samp")
    n = lax.axis_size("pair") * samp
    half = PANEL // samp
    s_dev = dosage.shape[0]
    width = PANEL + half + LANES
    kinds = phenotype.shape[0] * perms.shape[0]
    vmem = pl.BlockSpec(memory_space=pltpu.VMEM)
    hbm = pl.BlockSpec(memory_space=pltpu.HBM)
    kept_bytes = 4 * n * s_dev * width + 2 * dosage.size + (2 << 20)
    work_bytes = 64 * n * s_dev * PANEL + 4 * kinds * PANEL * half + (8 << 20)
    received = pl.pallas_call(
        functools.partial(exchange, n, samp),
        out_shape=jax.ShapeDtypeStruct((n, s_dev, width), jnp.bfloat16),
        in_specs=[hbm, hbm, hbm],
        out_specs=pl.BlockSpec(memory_space=pl.ANY),
        scratch_shapes=[
            pltpu.SMEM((2, pairs.shape[0]), jnp.int32),
            pltpu.VMEM(dosage.shape, dosage.dtype),
            pltpu.VMEM(phenotype.shape, phenotype.dtype),
            pltpu.VMEM((n, s_dev, width), jnp.bfloat16),
            pltpu.SemaphoreType.DMA((3,)),
            pltpu.SemaphoreType.DMA,
            pltpu.SemaphoreType.DMA,
        ],
        compiler_params=pltpu.CompilerParams(
            collective_id=0, has_side_effects=True, vmem_limit_bytes=min(kept_bytes, 60 << 20)
        ),
        name="exchange",
    )(pairs.T, dosage, phenotype)
    return pl.pallas_call(
        functools.partial(statistics, half),
        out_shape=jax.ShapeDtypeStruct((1, kinds, PANEL, half), jnp.bfloat16),
        in_specs=[vmem, vmem],
        out_specs=pl.BlockSpec(memory_space=pl.ANY),
        scratch_shapes=[
            pltpu.VMEM((kinds, PANEL, half), jnp.bfloat16),
            pltpu.SemaphoreType.DMA((kinds,)),
        ],
        compiler_params=pltpu.CompilerParams(vmem_limit_bytes=min(work_bytes, 60 << 20)),
        name="statistics",
    )(perms, received)


def solution(mesh):
    placed = (P(("rep", "pair", "samp"), None), P(None, ("rep", "pair", "samp")), P(), P())
    return jax.shard_map(
        on_device,
        mesh=mesh,
        in_specs=placed,
        out_specs=P(("rep", "pair"), None, None, "samp"),
        check_vma=False,
    )
```

```python
import functools

import jax
import jax.numpy as jnp
from jax import lax
from jax.experimental import pallas as pl
from jax.experimental.pallas import tpu as pltpu
from jax.sharding import PartitionSpec as P

PANEL = 512
LANES = 128


def partner(me, m, n):
    if n & (n - 1):
        return lax.rem(me + m, n)
    dest, weight = 0, 1
    while weight < n:
        dest = dest + (me // weight + m // weight) % 2 * weight
        weight *= 2
    return dest


def exchange(
    n, samp, pairs_hbm, dosage_hbm, pheno_hbm, out_ref,
    pairs_ref, dosage_ref, pheno_ref, send_buf, in_sems, send_sem, recv_sem,
):
    half = PANEL // samp
    me = lax.axis_index("pair") * samp + lax.axis_index("samp")
    s_dev = dosage_ref.shape[0]

    inputs = [
        pltpu.make_async_copy(dosage_hbm, dosage_ref, in_sems.at[0]),
        pltpu.make_async_copy(pheno_hbm, pheno_ref, in_sems.at[1]),
        pltpu.make_async_copy(pairs_hbm, pairs_ref, in_sems.at[2]),
    ]
    for copy in inputs:
        copy.start()
    barrier = pltpu.get_barrier_semaphore()

    def greet(i, carry):
        dest = partner(me, n - 1 - i, n)
        pl.semaphore_signal(
            barrier, inc=1, device_id={"pair": dest // samp, "samp": dest % samp},
            device_id_type=pl.DeviceIdType.MESH,
        )
        return carry

    lax.fori_loop(0, n - 1, greet, 0, unroll=n <= 16)
    for copy in inputs:
        copy.wait()

    row = lax.broadcasted_iota(jnp.int32, (s_dev, s_dev), 0)
    col = lax.broadcasted_iota(jnp.int32, (s_dev, s_dev), 1)
    lane = lax.broadcasted_iota(jnp.int32, (s_dev, LANES), 1)
    tail = jnp.zeros((s_dev, LANES), jnp.float32)
    for g in range(pheno_ref.shape[0]):
        values = pheno_ref[...].astype(jnp.float32)[g : g + 1, :]
        column = jnp.sum(jnp.where(row == col, values, 0.0), axis=1, keepdims=True)
        tail = jnp.where(lane == g, column, tail)
    tail = tail.astype(jnp.bfloat16)

    panels = dosage_ref.shape[1] // PANEL

    def fill(b, carry):
        first = jnp.full((s_dev, PANEL), pairs_ref[0, b], jnp.int32)
        second = jnp.full((s_dev, PANEL), pairs_ref[1, b], jnp.int32)

        def pick(p, kept):
            at = p * PANEL if isinstance(p, int) else pl.multiple_of(p * PANEL, PANEL)
            panel = dosage_ref[:, pl.ds(at, PANEL)].astype(jnp.float32)
            return jnp.where(first == p, panel, kept[0]), jnp.where(second == p, panel, kept[1])

        kept = (jnp.zeros((s_dev, PANEL), jnp.float32),) * 2
        if panels <= 16:
            for p in range(panels):
                kept = pick(p, kept)
        else:
            kept = lax.fori_loop(0, panels, pick, kept)
        geno_a, geno_b = (x.astype(jnp.bfloat16) for x in kept)
        for c in range(samp):
            send_buf[b * samp + c, :, :PANEL] = geno_a
            send_buf[b * samp + c, :, PANEL : PANEL + half] = geno_b[:, c * half : (c + 1) * half]
            send_buf[b * samp + c, :, PANEL + half :] = tail
        return carry

    lax.fori_loop(0, n // samp, fill, 0)
    pl.semaphore_wait(barrier, n - 1)

    def send(i, carry):
        dest = partner(me, n - 1 - i, n)
        pltpu.make_async_remote_copy(
            src_ref=send_buf.at[dest],
            dst_ref=out_ref.at[me],
            send_sem=send_sem,
            recv_sem=recv_sem,
            device_id={"pair": dest // samp, "samp": dest % samp},
            device_id_type=pl.DeviceIdType.MESH,
        ).start()
        return carry

    lax.fori_loop(0, n - 1, send, 0, unroll=n <= 16)
    pltpu.make_async_copy(send_buf.at[me], out_ref.at[me], recv_sem).start()
    pltpu.make_async_copy(out_ref, out_ref, recv_sem).wait()
    rest = send_buf.at[pl.ds(0, n - 1)]
    pltpu.make_async_copy(rest, rest, send_sem).wait()


def statistics(half, perms_ref, recv_ref, out_ref, tiles, sems):
    n, s_dev, _ = recv_ref.shape
    count = n * s_dev
    genes = tiles.shape[0] // perms_ref.shape[0]
    perms_n = perms_ref.shape[0]
    rows = jnp.concatenate([recv_ref[i].astype(jnp.float32) for i in range(n)], axis=0)
    geno_a = rows[:, :PANEL]
    geno_b = rows[:, PANEL : PANEL + half]
    pheno = rows[:, PANEL + half :].T[:8].astype(jnp.bfloat16)

    a_twice = jnp.concatenate([geno_a, geno_a], axis=0).T
    a_low = a_twice.astype(jnp.bfloat16)

    marg_b = jnp.sum(geno_b, axis=0, keepdims=True)
    centred = (geno_b - marg_b * (1.0 / count)) * (1.0 / count**0.5)
    high = centred.astype(jnp.bfloat16)
    low = (centred - high.astype(jnp.float32)).astype(jnp.bfloat16)
    b_split = jnp.concatenate([high, low], axis=0)

    sample = lax.broadcasted_iota(jnp.int32, (count, 2 * count), 0)
    picked = []
    for r in range(perms_n):
        order = perms_ref[r : r + 1, :]
        order = jnp.concatenate([order, order], axis=1)
        hot = jnp.where(sample == order, 1.0, 0.0).astype(jnp.bfloat16)
        picked.append(jnp.dot(pheno, hot, preferred_element_type=jnp.float32))
    slopes = [
        jnp.dot(picked[r].astype(jnp.bfloat16), b_split, preferred_element_type=jnp.float32)
        * (-1.0 / count)
        for r in range(perms_n)
    ]
    copies = []
    for k in range(genes * perms_n):
        g, r = k // perms_n, k % perms_n
        y = picked[r][g : g + 1, :]
        scaled = (a_twice * y).astype(jnp.bfloat16)
        slope = slopes[r][g : g + 1, :]
        slope_high = slope.astype(jnp.bfloat16).astype(jnp.float32)
        slope_low = slope - slope_high
        slope_rows = jnp.concatenate(
            [
                jnp.broadcast_to(slope_high, (count, half)),
                jnp.broadcast_to(slope_low, (count, half)),
            ],
            axis=0,
        ).astype(jnp.bfloat16)
        left = jnp.concatenate([scaled, a_low], axis=1)
        right = jnp.concatenate([b_split, slope_rows], axis=0)
        tiles[k] = jnp.dot(left, right, preferred_element_type=jnp.float32).astype(jnp.bfloat16)
        copy = pltpu.make_async_copy(tiles.at[k], out_ref.at[0, k], sems.at[k])
        copy.start()
        copies.append(copy)
    for copy in copies:
        copy.wait()


def on_device(dosage, phenotype, perms, pairs):
    samp = lax.axis_size("samp")
    n = lax.axis_size("pair") * samp
    half = PANEL // samp
    s_dev = dosage.shape[0]
    width = PANEL + half + LANES
    kinds = phenotype.shape[0] * perms.shape[0]
    vmem = pl.BlockSpec(memory_space=pltpu.VMEM)
    hbm = pl.BlockSpec(memory_space=pltpu.HBM)
    kept_bytes = 4 * n * s_dev * width + 2 * dosage.size + (2 << 20)
    work_bytes = 64 * n * s_dev * PANEL + 4 * kinds * PANEL * half + (8 << 20)
    received = pl.pallas_call(
        functools.partial(exchange, n, samp),
        out_shape=jax.ShapeDtypeStruct((n, s_dev, width), jnp.bfloat16),
        in_specs=[hbm, hbm, hbm],
        out_specs=pl.BlockSpec(memory_space=pl.ANY),
        scratch_shapes=[
            pltpu.SMEM((2, pairs.shape[0]), jnp.int32),
            pltpu.VMEM(dosage.shape, dosage.dtype),
            pltpu.VMEM(phenotype.shape, phenotype.dtype),
            pltpu.VMEM((n, s_dev, width), jnp.bfloat16),
            pltpu.SemaphoreType.DMA((3,)),
            pltpu.SemaphoreType.DMA,
            pltpu.SemaphoreType.DMA,
        ],
        compiler_params=pltpu.CompilerParams(
            collective_id=0, has_side_effects=True, vmem_limit_bytes=min(kept_bytes, 60 << 20)
        ),
        name="exchange",
    )(*(pltpu.with_memory_space_constraint(x, pltpu.HBM) for x in (pairs.T, dosage, phenotype)))
    return pl.pallas_call(
        functools.partial(statistics, half),
        out_shape=jax.ShapeDtypeStruct((1, kinds, PANEL, half), jnp.bfloat16),
        in_specs=[vmem, vmem],
        out_specs=pl.BlockSpec(memory_space=pl.ANY),
        scratch_shapes=[
            pltpu.VMEM((kinds, PANEL, half), jnp.bfloat16),
            pltpu.SemaphoreType.DMA((kinds,)),
        ],
        compiler_params=pltpu.CompilerParams(vmem_limit_bytes=min(work_bytes, 60 << 20)),
        name="statistics",
    )(perms, received)


def solution(mesh):
    placed = (P(("rep", "pair", "samp"), None), P(None, ("rep", "pair", "samp")), P(), P())
    return jax.shard_map(
        on_device,
        mesh=mesh,
        in_specs=placed,
        out_specs=P(("rep", "pair"), None, None, "samp"),
        check_vma=False,
    )
```

```python
import functools

import jax
import jax.numpy as jnp
from jax import lax
from jax.experimental import pallas as pl
from jax.experimental.pallas import tpu as pltpu
from jax.sharding import PartitionSpec as P

PANEL = 512
LANES = 128


def partner(me, m, n):
    if n & (n - 1):
        return lax.rem(me + m, n)
    dest, weight = 0, 1
    while weight < n:
        dest = dest + (me // weight + m // weight) % 2 * weight
        weight *= 2
    return dest


def exchange(
    n, samp, pairs_hbm, dosage_hbm, pheno_hbm, out_ref,
    pairs_ref, dosage_ref, pheno_ref, send_buf, in_sems, send_sem, recv_sem,
):
    half = PANEL // samp
    me = lax.axis_index("pair") * samp + lax.axis_index("samp")
    s_dev = dosage_ref.shape[0]

    inputs = [
        pltpu.make_async_copy(dosage_hbm, dosage_ref, in_sems.at[0]),
        pltpu.make_async_copy(pheno_hbm, pheno_ref, in_sems.at[1]),
        pltpu.make_async_copy(pairs_hbm, pairs_ref, in_sems.at[2]),
    ]
    for copy in inputs:
        copy.start()
    barrier = pltpu.get_barrier_semaphore()

    def greet(i, carry):
        dest = partner(me, n - 1 - i, n)
        pl.semaphore_signal(
            barrier, inc=1, device_id={"pair": dest // samp, "samp": dest % samp},
            device_id_type=pl.DeviceIdType.MESH,
        )
        return carry

    lax.fori_loop(0, n - 1, greet, 0, unroll=n <= 16)
    for copy in inputs:
        copy.wait()

    row = lax.broadcasted_iota(jnp.int32, (s_dev, s_dev), 0)
    col = lax.broadcasted_iota(jnp.int32, (s_dev, s_dev), 1)
    lane = lax.broadcasted_iota(jnp.int32, (s_dev, LANES), 1)
    tail = jnp.zeros((s_dev, LANES), jnp.float32)
    for g in range(pheno_ref.shape[0]):
        values = pheno_ref[...].astype(jnp.float32)[g : g + 1, :]
        column = jnp.sum(jnp.where(row == col, values, 0.0), axis=1, keepdims=True)
        tail = jnp.where(lane == g, column, tail)
    tail = tail.astype(jnp.bfloat16)

    panels = dosage_ref.shape[1] // PANEL
    pair_me, samp_me = lax.axis_index("pair"), lax.axis_index("samp")
    pair_n = n // samp
    small = panels <= 16
    if small:
        whole = dosage_ref[...].astype(jnp.float32)

    def fill(i):
        b = partner(pair_me, pair_n - 1 - i, pair_n)
        first = jnp.full((s_dev, LANES), pairs_ref[0, b], jnp.int32)
        second = jnp.full((s_dev, LANES), pairs_ref[1, b], jnp.int32)
        tiles = PANEL // LANES

        def pick(p, kept):
            if small:
                found = [whole[:, p * PANEL + t * LANES :][:, :LANES] for t in range(tiles)]
            else:
                panel = dosage_ref[:, pl.ds(pl.multiple_of(p * PANEL, PANEL), PANEL)]
                found = [
                    panel[:, t * LANES : (t + 1) * LANES].astype(jnp.float32) for t in range(tiles)
                ]
            in_a, in_b = first == p, second == p
            return (
                tuple(jnp.where(in_a, x, old) for x, old in zip(found, kept[0])),
                tuple(jnp.where(in_b, x, old) for x, old in zip(found, kept[1])),
            )

        kept = ((jnp.zeros((s_dev, LANES), jnp.float32),) * tiles,) * 2
        if small:
            for p in range(panels):
                kept = pick(p, kept)
        else:
            kept = lax.fori_loop(0, panels, pick, kept)
        geno_a, geno_b = (jnp.concatenate(x, axis=1).astype(jnp.bfloat16) for x in kept)
        for c in range(samp):
            send_buf[b * samp + c, :, :PANEL] = geno_a
            send_buf[b * samp + c, :, PANEL : PANEL + half] = geno_b[:, c * half : (c + 1) * half]
            send_buf[b * samp + c, :, PANEL + half :] = tail

    def send(b, c):
        pltpu.make_async_remote_copy(
            src_ref=send_buf.at[b * samp + c],
            dst_ref=out_ref.at[me],
            send_sem=send_sem,
            recv_sem=recv_sem,
            device_id={"pair": b, "samp": c},
            device_id_type=pl.DeviceIdType.MESH,
        ).start()

    fill(0)
    pl.semaphore_wait(barrier, n - 1)

    def step(i, carry):
        fill(i + 1)
        b = partner(pair_me, pair_n - 1 - i, pair_n)
        for c in range(samp):
            send(b, c)
        return carry

    if small:
        for i in range(pair_n - 1):
            step(i, 0)
    else:
        lax.fori_loop(0, pair_n - 1, step, 0)
    for c in range(1, samp):
        send(pair_me, lax.rem(samp_me + c, samp))
    pltpu.make_async_copy(send_buf.at[me], out_ref.at[me], recv_sem).start()
    pltpu.make_async_copy(out_ref, out_ref, recv_sem).wait()
    rest = send_buf.at[pl.ds(0, n - 1)]
    pltpu.make_async_copy(rest, rest, send_sem).wait()


def statistics(half, perms_ref, recv_ref, out_ref, tiles, sems):
    n, s_dev, _ = recv_ref.shape
    count = n * s_dev
    genes = tiles.shape[0] // perms_ref.shape[0]
    perms_n = perms_ref.shape[0]
    rows = jnp.concatenate([recv_ref[i].astype(jnp.float32) for i in range(n)], axis=0)
    geno_a = rows[:, :PANEL]
    geno_b = rows[:, PANEL : PANEL + half]
    pheno = rows[:, PANEL + half :].T[:8].astype(jnp.bfloat16)

    a_twice = jnp.concatenate([geno_a, geno_a], axis=0).T
    a_low = a_twice.astype(jnp.bfloat16)

    marg_b = jnp.sum(geno_b, axis=0, keepdims=True)
    centred = (geno_b - marg_b * (1.0 / count)) * (1.0 / count**0.5)
    high = centred.astype(jnp.bfloat16)
    low = (centred - high.astype(jnp.float32)).astype(jnp.bfloat16)
    b_split = jnp.concatenate([high, low], axis=0)

    sample = lax.broadcasted_iota(jnp.int32, (count, 2 * count), 0)
    picked = []
    for r in range(perms_n):
        order = perms_ref[r : r + 1, :]
        order = jnp.concatenate([order, order], axis=1)
        hot = jnp.where(sample == order, 1.0, 0.0).astype(jnp.bfloat16)
        picked.append(jnp.dot(pheno, hot, preferred_element_type=jnp.float32))
    slopes = [
        jnp.dot(picked[r].astype(jnp.bfloat16), b_split, preferred_element_type=jnp.float32)
        * (-1.0 / count)
        for r in range(perms_n)
    ]
    copies = []
    for k in range(genes * perms_n):
        g, r = k // perms_n, k % perms_n
        y = picked[r][g : g + 1, :]
        scaled = (a_twice * y).astype(jnp.bfloat16)
        slope = slopes[r][g : g + 1, :]
        slope_high = slope.astype(jnp.bfloat16).astype(jnp.float32)
        slope_low = slope - slope_high
        slope_rows = jnp.concatenate(
            [
                jnp.broadcast_to(slope_high, (count, half)),
                jnp.broadcast_to(slope_low, (count, half)),
            ],
            axis=0,
        ).astype(jnp.bfloat16)
        left = jnp.concatenate([scaled, a_low], axis=1)
        right = jnp.concatenate([b_split, slope_rows], axis=0)
        tiles[k] = jnp.dot(left, right, preferred_element_type=jnp.float32).astype(jnp.bfloat16)
        copy = pltpu.make_async_copy(tiles.at[k], out_ref.at[0, k], sems.at[k])
        copy.start()
        copies.append(copy)
    for copy in copies:
        copy.wait()


def on_device(dosage, phenotype, perms, pairs):
    samp = lax.axis_size("samp")
    n = lax.axis_size("pair") * samp
    half = PANEL // samp
    s_dev = dosage.shape[0]
    width = PANEL + half + LANES
    kinds = phenotype.shape[0] * perms.shape[0]
    vmem = pl.BlockSpec(memory_space=pltpu.VMEM)
    hbm = pl.BlockSpec(memory_space=pltpu.HBM)
    kept_bytes = 4 * n * s_dev * width + 2 * dosage.size + (2 << 20)
    work_bytes = 64 * n * s_dev * PANEL + 4 * kinds * PANEL * half + (8 << 20)
    received = pl.pallas_call(
        functools.partial(exchange, n, samp),
        out_shape=jax.ShapeDtypeStruct((n, s_dev, width), jnp.bfloat16),
        in_specs=[hbm, hbm, hbm],
        out_specs=pl.BlockSpec(memory_space=pl.ANY),
        scratch_shapes=[
            pltpu.SMEM((2, pairs.shape[0]), jnp.int32),
            pltpu.VMEM(dosage.shape, dosage.dtype),
            pltpu.VMEM(phenotype.shape, phenotype.dtype),
            pltpu.VMEM((n, s_dev, width), jnp.bfloat16),
            pltpu.SemaphoreType.DMA((3,)),
            pltpu.SemaphoreType.DMA,
            pltpu.SemaphoreType.DMA,
        ],
        compiler_params=pltpu.CompilerParams(
            collective_id=0, has_side_effects=True, vmem_limit_bytes=min(kept_bytes, 60 << 20)
        ),
        name="exchange",
    )(*(pltpu.with_memory_space_constraint(x, pltpu.HBM) for x in (pairs.T, dosage, phenotype)))
    return pl.pallas_call(
        functools.partial(statistics, half),
        out_shape=jax.ShapeDtypeStruct((1, kinds, PANEL, half), jnp.bfloat16),
        in_specs=[vmem, vmem],
        out_specs=pl.BlockSpec(memory_space=pl.ANY),
        scratch_shapes=[
            pltpu.VMEM((kinds, PANEL, half), jnp.bfloat16),
            pltpu.SemaphoreType.DMA((kinds,)),
        ],
        compiler_params=pltpu.CompilerParams(vmem_limit_bytes=min(work_bytes, 60 << 20)),
        name="statistics",
    )(perms, received)


def solution(mesh):
    placed = (P(("rep", "pair", "samp"), None), P(None, ("rep", "pair", "samp")), P(), P())
    return jax.shard_map(
        on_device,
        mesh=mesh,
        in_specs=placed,
        out_specs=P(("rep", "pair"), None, None, "samp"),
        check_vma=False,
    )
```

```python
import functools

import jax
import jax.numpy as jnp
from jax import lax
from jax.experimental import pallas as pl
from jax.experimental.pallas import tpu as pltpu
from jax.sharding import PartitionSpec as P

PANEL = 512
LANES = 128
CHUNKS = 2


def partner(me, m, n):
    if n & (n - 1):
        return lax.rem(me + m, n)
    dest, weight = 0, 1
    while weight < n:
        dest = dest + (me // weight + m // weight) % 2 * weight
        weight *= 2
    return dest


def exchange(
    n, samp, pairs_hbm, dosage_hbm, pheno_hbm, perms_hbm, out_ref, y_ref, hot_ref,
    pairs_ref, perms_ref, dosage_ref, pheno_ref, send_buf, own_y, in_sems, send_sem, recv_sem, y_send, y_recv,
):
    half = PANEL // samp
    me = lax.axis_index("pair") * samp + lax.axis_index("samp")
    s_dev = dosage_ref.shape[0]

    inputs = [
        pltpu.make_async_copy(dosage_hbm, dosage_ref, in_sems.at[0]),
        pltpu.make_async_copy(pheno_hbm, pheno_ref, in_sems.at[1]),
        pltpu.make_async_copy(pairs_hbm, pairs_ref, in_sems.at[2]),
        pltpu.make_async_copy(perms_hbm, perms_ref, in_sems.at[3]),
    ]
    for copy in inputs:
        copy.start()
    barrier = pltpu.get_barrier_semaphore()

    def greet(i, carry):
        dest = partner(me, n - 1 - i, n)
        pl.semaphore_signal(
            barrier, inc=1, device_id={"pair": dest // samp, "samp": dest % samp},
            device_id_type=pl.DeviceIdType.MESH,
        )
        return carry

    lax.fori_loop(0, n - 1, greet, 0, unroll=n <= 16)
    for copy in inputs:
        copy.wait()

    lane = lax.broadcasted_iota(jnp.int32, own_y.shape, 1)
    values = pheno_ref[...].astype(jnp.float32)
    placed = jnp.zeros(own_y.shape, jnp.float32)
    for i in range(s_dev):
        placed = jnp.where(lane == me * s_dev + i, values[:, i : i + 1], placed)
    own_y[...] = placed.astype(jnp.bfloat16)

    panels = dosage_ref.shape[1] // PANEL
    pair_me, samp_me = lax.axis_index("pair"), lax.axis_index("samp")
    pair_n = n // samp
    small = panels <= 16
    if small:
        whole = dosage_ref[...].astype(jnp.float32)

    def fill(i):
        b = partner(pair_me, pair_n - 1 - i, pair_n)
        first = jnp.full((s_dev, LANES), pairs_ref[0, b], jnp.int32)
        second = jnp.full((s_dev, LANES), pairs_ref[1, b], jnp.int32)
        tiles = PANEL // LANES

        def pick(p, kept):
            if small:
                found = [whole[:, p * PANEL + t * LANES :][:, :LANES] for t in range(tiles)]
            else:
                panel = dosage_ref[:, pl.ds(pl.multiple_of(p * PANEL, PANEL), PANEL)]
                found = [
                    panel[:, t * LANES : (t + 1) * LANES].astype(jnp.float32) for t in range(tiles)
                ]
            in_a, in_b = first == p, second == p
            return (
                tuple(jnp.where(in_a, x, old) for x, old in zip(found, kept[0])),
                tuple(jnp.where(in_b, x, old) for x, old in zip(found, kept[1])),
            )

        kept = ((jnp.zeros((s_dev, LANES), jnp.float32),) * tiles,) * 2
        if small:
            for p in range(panels):
                kept = pick(p, kept)
        else:
            kept = lax.fori_loop(0, panels, pick, kept)
        geno_a, geno_b = (jnp.concatenate(x, axis=1).astype(jnp.bfloat16) for x in kept)
        for c in range(samp):
            send_buf[b * samp + c, :, :PANEL] = geno_a
            send_buf[b * samp + c, :, PANEL : PANEL + half] = geno_b[:, c * half : (c + 1) * half]

    def send(b, c):
        pltpu.make_async_remote_copy(
            src_ref=send_buf.at[b * samp + c],
            dst_ref=out_ref.at[me],
            send_sem=send_sem,
            recv_sem=recv_sem,
            device_id={"pair": b, "samp": c},
            device_id_type=pl.DeviceIdType.MESH,
        ).start()
        pltpu.make_async_remote_copy(
            src_ref=own_y,
            dst_ref=y_ref.at[me],
            send_sem=y_send,
            recv_sem=y_recv,
            device_id={"pair": b, "samp": c},
            device_id_type=pl.DeviceIdType.MESH,
        ).start()

    fill(0)
    pl.semaphore_wait(barrier, n - 1)

    def step(i, carry):
        fill(i + 1)
        b = partner(pair_me, pair_n - 1 - i, pair_n)
        for c in range(samp):
            send(b, c)
        return carry

    if small:
        for i in range(pair_n - 1):
            step(i, 0)
    else:
        lax.fori_loop(0, pair_n - 1, step, 0)
    for c in range(1, samp):
        send(pair_me, lax.rem(samp_me + c, samp))
    pltpu.make_async_copy(send_buf.at[me], out_ref.at[me], recv_sem).start()
    pltpu.make_async_copy(own_y, y_ref.at[me], y_recv).start()

    count = hot_ref.shape[1]
    sample = lax.broadcasted_iota(jnp.int32, (count, 2 * count), 0)
    for r in range(perms_ref.shape[0]):
        order = perms_ref[r : r + 1, :]
        order = jnp.concatenate([order, order], axis=1)
        hot_ref[r] = jnp.where(sample == order, 1.0, 0.0).astype(jnp.bfloat16)

    pltpu.make_async_copy(out_ref, out_ref, recv_sem).wait()
    pltpu.make_async_copy(y_ref, y_ref, y_recv).wait()
    for buf, sem in ((send_buf, send_sem), (y_ref, y_send)):
        rest = buf.at[pl.ds(0, n - 1)]
        pltpu.make_async_copy(rest, rest, sem).wait()


def statistics(half, recv_ref, y_ref, hot_ref, out_ref, tiles, sems):
    n, s_dev, _ = recv_ref.shape
    count = n * s_dev
    perms_n = hot_ref.shape[0]
    genes = tiles.shape[0] // perms_n
    rows = jnp.concatenate([recv_ref[i].astype(jnp.float32) for i in range(n)], axis=0)
    geno_a = rows[:, :PANEL]
    geno_b = rows[:, PANEL : PANEL + half]
    pheno = jnp.sum(y_ref[...].astype(jnp.float32), axis=0)[:, :count]
    pheno = jnp.concatenate([pheno] * (8 // genes), axis=0).astype(jnp.bfloat16)

    a_twice = jnp.concatenate([geno_a, geno_a], axis=0).T
    a_low = a_twice.astype(jnp.bfloat16)

    marg_b = jnp.sum(geno_b, axis=0, keepdims=True)
    centred = (geno_b - marg_b * (1.0 / count)) * (1.0 / count**0.5)
    high = centred.astype(jnp.bfloat16)
    low = (centred - high.astype(jnp.float32)).astype(jnp.bfloat16)
    b_split = jnp.concatenate([high, low], axis=0)

    picked = [
        jnp.dot(pheno, hot_ref[r], preferred_element_type=jnp.float32) for r in range(perms_n)
    ]
    slopes = [
        jnp.dot(picked[r].astype(jnp.bfloat16), b_split, preferred_element_type=jnp.float32)
        * (-1.0 / count)
        for r in range(perms_n)
    ]
    copies = []
    for k in range(genes * perms_n):
        g, r = k // perms_n, k % perms_n
        y = picked[r][g : g + 1, :]
        scaled = (a_twice * y).astype(jnp.bfloat16)
        slope = slopes[r][g : g + 1, :]
        slope_high = slope.astype(jnp.bfloat16).astype(jnp.float32)
        slope_low = slope - slope_high
        slope_rows = jnp.concatenate(
            [
                jnp.broadcast_to(slope_high, (count, half)),
                jnp.broadcast_to(slope_low, (count, half)),
            ],
            axis=0,
        ).astype(jnp.bfloat16)
        left = jnp.concatenate([scaled, a_low], axis=1)
        right = jnp.concatenate([b_split, slope_rows], axis=0)
        for part in range(CHUNKS):
            at = pl.ds(part * PANEL // CHUNKS, PANEL // CHUNKS)
            block = left[part * PANEL // CHUNKS : (part + 1) * PANEL // CHUNKS]
            value = jnp.dot(block, right, preferred_element_type=jnp.float32)
            tiles[k, at] = value.astype(jnp.bfloat16)
            copy = pltpu.make_async_copy(
                tiles.at[k, at], out_ref.at[0, k, at], sems.at[k * CHUNKS + part]
            )
            copy.start()
            copies.append(copy)
    for copy in copies:
        copy.wait()


def on_device(dosage, phenotype, perms, pairs):
    samp = lax.axis_size("samp")
    n = lax.axis_size("pair") * samp
    half = PANEL // samp
    s_dev = dosage.shape[0]
    count = n * s_dev
    width = PANEL + half
    y_shape = (phenotype.shape[0], pl.cdiv(n * s_dev, LANES) * LANES)
    kinds = phenotype.shape[0] * perms.shape[0]
    vmem = pl.BlockSpec(memory_space=pltpu.VMEM)
    hbm = pl.BlockSpec(memory_space=pltpu.HBM)
    kept_bytes = 4 * n * s_dev * width + 2 * dosage.size + 16 * count * count + (2 << 20)
    work_bytes = 64 * n * s_dev * PANEL + 4 * kinds * PANEL * half + (8 << 20)
    received = pl.pallas_call(
        functools.partial(exchange, n, samp),
        out_shape=[
            jax.ShapeDtypeStruct((n, s_dev, width), jnp.bfloat16),
            jax.ShapeDtypeStruct((n, *y_shape), jnp.bfloat16),
            jax.ShapeDtypeStruct((perms.shape[0], count, 2 * count), jnp.bfloat16),
        ],
        in_specs=[hbm] * 4,
        out_specs=[pl.BlockSpec(memory_space=pl.ANY)] * 2 + [vmem],
        scratch_shapes=[
            pltpu.SMEM((2, pairs.shape[0]), jnp.int32),
            pltpu.VMEM(perms.shape, jnp.int32),
            pltpu.VMEM(dosage.shape, dosage.dtype),
            pltpu.VMEM(phenotype.shape, phenotype.dtype),
            pltpu.VMEM((n, s_dev, width), jnp.bfloat16),
            pltpu.VMEM(y_shape, jnp.bfloat16),
            pltpu.SemaphoreType.DMA((4,)),
            pltpu.SemaphoreType.DMA,
            pltpu.SemaphoreType.DMA,
            pltpu.SemaphoreType.DMA,
            pltpu.SemaphoreType.DMA,
        ],
        compiler_params=pltpu.CompilerParams(
            collective_id=0, has_side_effects=True, vmem_limit_bytes=min(kept_bytes, 60 << 20)
        ),
        name="exchange",
    )(*(pltpu.with_memory_space_constraint(x, pltpu.HBM) for x in (pairs.T, dosage, phenotype, perms)))
    return pl.pallas_call(
        functools.partial(statistics, half),
        out_shape=jax.ShapeDtypeStruct((1, kinds, PANEL, half), jnp.bfloat16),
        in_specs=[vmem] * 3,
        out_specs=pl.BlockSpec(memory_space=pl.ANY),
        scratch_shapes=[
            pltpu.VMEM((kinds, PANEL, half), jnp.bfloat16),
            pltpu.SemaphoreType.DMA((kinds * CHUNKS,)),
        ],
        compiler_params=pltpu.CompilerParams(vmem_limit_bytes=min(work_bytes, 60 << 20)),
        name="statistics",
    )(*received)


def solution(mesh):
    placed = (P(("rep", "pair", "samp"), None), P(None, ("rep", "pair", "samp")), P(), P())
    return jax.shard_map(
        on_device,
        mesh=mesh,
        in_specs=placed,
        out_specs=P(("rep", "pair"), None, None, "samp"),
        check_vma=False,
    )
```

```python
import functools

import jax
import jax.numpy as jnp
from jax import lax
from jax.experimental import pallas as pl
from jax.experimental.pallas import tpu as pltpu
from jax.sharding import PartitionSpec as P

PANEL = 512
LANES = 128
CHUNKS = 2


def partner(me, m, n):
    if n & (n - 1):
        return lax.rem(me + m, n)
    dest, weight = 0, 1
    while weight < n:
        dest = dest + (me // weight + m // weight) % 2 * weight
        weight *= 2
    return dest


def exchange(
    n, samp, pairs_hbm, dosage_hbm, pheno_hbm, perms_hbm, out_ref, y_ref, hot_ref,
    pairs_ref, perms_ref, dosage_ref, pheno_ref, send_buf, own_y, in_sems, send_sem, recv_sem, y_send, y_recv, far_sems,
):
    half = PANEL // samp
    me = lax.axis_index("pair") * samp + lax.axis_index("samp")
    s_dev = dosage_ref.shape[0]

    inputs = [
        pltpu.make_async_copy(dosage_hbm, dosage_ref, in_sems.at[0]),
        pltpu.make_async_copy(pheno_hbm, pheno_ref, in_sems.at[1]),
        pltpu.make_async_copy(pairs_hbm, pairs_ref, in_sems.at[2]),
        pltpu.make_async_copy(perms_hbm, perms_ref, in_sems.at[3]),
    ]
    for copy in inputs:
        copy.start()
    barrier = pltpu.get_barrier_semaphore()

    def greet(i, carry):
        dest = partner(me, n - 1 - i, n)
        pl.semaphore_signal(
            barrier, inc=1, device_id={"pair": dest // samp, "samp": dest % samp},
            device_id_type=pl.DeviceIdType.MESH,
        )
        return carry

    lax.fori_loop(0, n - 1, greet, 0, unroll=n <= 16)
    for copy in inputs:
        copy.wait()

    lane = lax.broadcasted_iota(jnp.int32, own_y.shape, 1)
    values = pheno_ref[...].astype(jnp.float32)
    placed = jnp.zeros(own_y.shape, jnp.float32)
    for i in range(s_dev):
        placed = jnp.where(lane == me * s_dev + i, values[:, i : i + 1], placed)
    own_y[...] = placed.astype(jnp.bfloat16)

    panels = dosage_ref.shape[1] // PANEL
    pair_me, samp_me = lax.axis_index("pair"), lax.axis_index("samp")
    pair_n = n // samp
    small = panels <= 16
    if small:
        whole = dosage_ref[...].astype(jnp.float32)

    def fill(i):
        b = partner(pair_me, pair_n - 1 - i, pair_n)
        first = jnp.full((s_dev, LANES), pairs_ref[0, b], jnp.int32)
        second = jnp.full((s_dev, LANES), pairs_ref[1, b], jnp.int32)
        tiles = PANEL // LANES

        def pick(p, kept):
            if small:
                found = [whole[:, p * PANEL + t * LANES :][:, :LANES] for t in range(tiles)]
            else:
                panel = dosage_ref[:, pl.ds(pl.multiple_of(p * PANEL, PANEL), PANEL)]
                found = [
                    panel[:, t * LANES : (t + 1) * LANES].astype(jnp.float32) for t in range(tiles)
                ]
            in_a, in_b = first == p, second == p
            return (
                tuple(jnp.where(in_a, x, old) for x, old in zip(found, kept[0])),
                tuple(jnp.where(in_b, x, old) for x, old in zip(found, kept[1])),
            )

        kept = ((jnp.zeros((s_dev, LANES), jnp.float32),) * tiles,) * 2
        if small:
            for p in range(panels):
                kept = pick(p, kept)
        else:
            kept = lax.fori_loop(0, panels, pick, kept)
        geno_a, geno_b = (jnp.concatenate(x, axis=1).astype(jnp.bfloat16) for x in kept)
        for c in range(samp):
            send_buf[b * samp + c, :, :PANEL] = geno_a
            send_buf[b * samp + c, :, PANEL : PANEL + half] = geno_b[:, c * half : (c + 1) * half]

    far = far_sems.shape[0]
    cells = pl.ds(PANEL, half)

    def reach(b, c, src, dst, sems):
        pltpu.make_async_remote_copy(
            src_ref=src,
            dst_ref=dst,
            send_sem=sems[0],
            recv_sem=sems[1],
            device_id={"pair": b, "samp": c},
            device_id_type=pl.DeviceIdType.MESH,
        ).start()

    def send(b, c, sem=None):
        reach(b, c, send_buf.at[b * samp + c], out_ref.at[me], (send_sem, recv_sem if sem is None else sem))
        reach(b, c, own_y, y_ref.at[me], (y_send, y_recv))

    def send_far(i, b):
        send(b, samp_me, far_sems.at[i])
        for c in range(1, samp):
            other = lax.rem(samp_me + c, samp)
            slab = send_buf.at[b * samp + other]
            reach(b, other, slab.at[:, cells], out_ref.at[me, :, cells], (send_sem, recv_sem))
            reach(b, other, own_y, y_ref.at[me], (y_send, y_recv))

    def pass_on(i, carry):
        back = i + 1 if pair_n & (pair_n - 1) else pair_n - 1 - i
        source = partner(pair_me, back, pair_n) * samp + samp_me
        slab = out_ref.at[source]
        pltpu.make_async_copy(slab, slab, far_sems.at[i]).wait()
        row = out_ref.at[source, :, pl.ds(0, PANEL)]
        for c in range(1, samp):
            reach(pair_me, lax.rem(samp_me + c, samp), row, row, (send_sem, recv_sem))
        return carry

    fill(0)
    pl.semaphore_wait(barrier, n - 1)

    def step(i, carry):
        fill(i + 1)
        b = partner(pair_me, pair_n - 1 - i, pair_n)
        for c in range(samp):
            send(b, c)
        return carry

    def far_step(i, carry):
        fill(i + 1)
        send_far(i, partner(pair_me, pair_n - 1 - i, pair_n))
        return carry

    if small:
        for i in range(pair_n - 1):
            (far_step if i < far else step)(i, 0)
    else:
        lax.fori_loop(0, far, far_step, 0)
        lax.fori_loop(far, pair_n - 1, step, 0)
    for c in range(1, samp):
        send(pair_me, lax.rem(samp_me + c, samp))
    pltpu.make_async_copy(send_buf.at[me], out_ref.at[me], recv_sem).start()
    pltpu.make_async_copy(own_y, y_ref.at[me], y_recv).start()

    count = hot_ref.shape[1]
    sample = lax.broadcasted_iota(jnp.int32, (count, 2 * count), 0)
    for r in range(perms_ref.shape[0]):
        order = perms_ref[r : r + 1, :]
        order = jnp.concatenate([order, order], axis=1)
        hot_ref[r] = jnp.where(sample == order, 1.0, 0.0).astype(jnp.bfloat16)

    lax.fori_loop(0, far, pass_on, 0)
    landed = out_ref.at[pl.ds(0, n - far)]
    pltpu.make_async_copy(landed, landed, recv_sem).wait()
    pltpu.make_async_copy(y_ref, y_ref, y_recv).wait()
    for buf, sem in ((send_buf, send_sem), (y_ref, y_send)):
        rest = buf.at[pl.ds(0, n - 1)]
        pltpu.make_async_copy(rest, rest, sem).wait()


def statistics(half, recv_ref, y_ref, hot_ref, out_ref, tiles, sems):
    n, s_dev, _ = recv_ref.shape
    count = n * s_dev
    perms_n = hot_ref.shape[0]
    genes = tiles.shape[0] // perms_n
    rows = jnp.concatenate([recv_ref[i].astype(jnp.float32) for i in range(n)], axis=0)
    geno_a = rows[:, :PANEL]
    geno_b = rows[:, PANEL : PANEL + half]
    pheno = jnp.sum(y_ref[...].astype(jnp.float32), axis=0)[:, :count]
    pheno = jnp.concatenate([pheno] * (8 // genes), axis=0).astype(jnp.bfloat16)

    a_twice = jnp.concatenate([geno_a, geno_a], axis=0).T
    a_low = a_twice.astype(jnp.bfloat16)

    marg_b = jnp.sum(geno_b, axis=0, keepdims=True)
    centred = (geno_b - marg_b * (1.0 / count)) * (1.0 / count**0.5)
    high = centred.astype(jnp.bfloat16)
    low = (centred - high.astype(jnp.float32)).astype(jnp.bfloat16)
    b_split = jnp.concatenate([high, low], axis=0)

    picked = [
        jnp.dot(pheno, hot_ref[r], preferred_element_type=jnp.float32) for r in range(perms_n)
    ]
    slopes = [
        jnp.dot(picked[r].astype(jnp.bfloat16), b_split, preferred_element_type=jnp.float32)
        * (-1.0 / count)
        for r in range(perms_n)
    ]
    copies = []
    for k in range(genes * perms_n):
        g, r = k // perms_n, k % perms_n
        y = picked[r][g : g + 1, :]
        scaled = (a_twice * y).astype(jnp.bfloat16)
        slope = slopes[r][g : g + 1, :]
        slope_high = slope.astype(jnp.bfloat16).astype(jnp.float32)
        slope_low = slope - slope_high
        slope_rows = jnp.concatenate(
            [
                jnp.broadcast_to(slope_high, (count, half)),
                jnp.broadcast_to(slope_low, (count, half)),
            ],
            axis=0,
        ).astype(jnp.bfloat16)
        left = jnp.concatenate([scaled, a_low], axis=1)
        right = jnp.concatenate([b_split, slope_rows], axis=0)
        for part in range(CHUNKS):
            at = pl.ds(part * PANEL // CHUNKS, PANEL // CHUNKS)
            block = left[part * PANEL // CHUNKS : (part + 1) * PANEL // CHUNKS]
            value = jnp.dot(block, right, preferred_element_type=jnp.float32)
            tiles[k, at] = value.astype(jnp.bfloat16)
            copy = pltpu.make_async_copy(
                tiles.at[k, at], out_ref.at[0, k, at], sems.at[k * CHUNKS + part]
            )
            copy.start()
            copies.append(copy)
    for copy in copies:
        copy.wait()


def on_device(dosage, phenotype, perms, pairs):
    samp = lax.axis_size("samp")
    n = lax.axis_size("pair") * samp
    half = PANEL // samp
    s_dev = dosage.shape[0]
    count = n * s_dev
    width = PANEL + half
    y_shape = (phenotype.shape[0], pl.cdiv(n * s_dev, LANES) * LANES)
    kinds = phenotype.shape[0] * perms.shape[0]
    vmem = pl.BlockSpec(memory_space=pltpu.VMEM)
    hbm = pl.BlockSpec(memory_space=pltpu.HBM)
    kept_bytes = 4 * n * s_dev * width + 2 * dosage.size + 16 * count * count + (2 << 20)
    work_bytes = 64 * n * s_dev * PANEL + 4 * kinds * PANEL * half + (8 << 20)
    received = pl.pallas_call(
        functools.partial(exchange, n, samp),
        out_shape=[
            jax.ShapeDtypeStruct((n, s_dev, width), jnp.bfloat16),
            jax.ShapeDtypeStruct((n, *y_shape), jnp.bfloat16),
            jax.ShapeDtypeStruct((perms.shape[0], count, 2 * count), jnp.bfloat16),
        ],
        in_specs=[hbm] * 4,
        out_specs=[pl.BlockSpec(memory_space=pl.ANY)] * 2 + [vmem],
        scratch_shapes=[
            pltpu.SMEM((2, pairs.shape[0]), jnp.int32),
            pltpu.VMEM(perms.shape, jnp.int32),
            pltpu.VMEM(dosage.shape, dosage.dtype),
            pltpu.VMEM(phenotype.shape, phenotype.dtype),
            pltpu.VMEM((n, s_dev, width), jnp.bfloat16),
            pltpu.VMEM(y_shape, jnp.bfloat16),
            pltpu.SemaphoreType.DMA((4,)),
            pltpu.SemaphoreType.DMA,
            pltpu.SemaphoreType.DMA,
            pltpu.SemaphoreType.DMA,
            pltpu.SemaphoreType.DMA,
            pltpu.SemaphoreType.DMA((max(1, n // samp // 4),)),
        ],
        compiler_params=pltpu.CompilerParams(
            collective_id=0, has_side_effects=True, vmem_limit_bytes=min(kept_bytes, 60 << 20)
        ),
        name="exchange",
    )(*(pltpu.with_memory_space_constraint(x, pltpu.HBM) for x in (pairs.T, dosage, phenotype, perms)))
    return pl.pallas_call(
        functools.partial(statistics, half),
        out_shape=jax.ShapeDtypeStruct((1, kinds, PANEL, half), jnp.bfloat16),
        in_specs=[vmem] * 3,
        out_specs=pl.BlockSpec(memory_space=pl.ANY),
        scratch_shapes=[
            pltpu.VMEM((kinds, PANEL, half), jnp.bfloat16),
            pltpu.SemaphoreType.DMA((kinds * CHUNKS,)),
        ],
        compiler_params=pltpu.CompilerParams(vmem_limit_bytes=min(work_bytes, 60 << 20)),
        name="statistics",
    )(*received)


def solution(mesh):
    placed = (P(("rep", "pair", "samp"), None), P(None, ("rep", "pair", "samp")), P(), P())
    return jax.shard_map(
        on_device,
        mesh=mesh,
        in_specs=placed,
        out_specs=P(("rep", "pair"), None, None, "samp"),
        check_vma=False,
    )
```

```python
import functools

import jax
import jax.numpy as jnp
from jax import lax
from jax.experimental import pallas as pl
from jax.experimental.pallas import tpu as pltpu
from jax.sharding import PartitionSpec as P

PANEL = 512
LANES = 128
CHUNKS = 2


def partner(me, m, n):
    if n & (n - 1):
        return lax.rem(me + m, n)
    dest, weight = 0, 1
    while weight < n:
        dest = dest + (me // weight + m // weight) % 2 * weight
        weight *= 2
    return dest


def exchange(
    n, samp, pairs_hbm, dosage_hbm, pheno_hbm, perms_hbm, out_ref, y_ref, hot_ref,
    pairs_ref, perms_ref, dosage_ref, pheno_ref, send_buf, own_y, in_sems, send_sem, recv_sem, y_send, y_recv, far_sems,
):
    half = PANEL // samp
    me = lax.axis_index("pair") * samp + lax.axis_index("samp")
    s_dev = dosage_ref.shape[0]

    inputs = [
        pltpu.make_async_copy(dosage_hbm, dosage_ref, in_sems.at[0]),
        pltpu.make_async_copy(pheno_hbm, pheno_ref, in_sems.at[1]),
        pltpu.make_async_copy(pairs_hbm, pairs_ref, in_sems.at[2]),
        pltpu.make_async_copy(perms_hbm, perms_ref, in_sems.at[3]),
    ]
    for copy in inputs:
        copy.start()
    barrier = pltpu.get_barrier_semaphore()

    def greet(i, carry):
        dest = partner(me, n - 1 - i, n)
        pl.semaphore_signal(
            barrier, inc=1, device_id={"pair": dest // samp, "samp": dest % samp},
            device_id_type=pl.DeviceIdType.MESH,
        )
        return carry

    lax.fori_loop(0, n - 1, greet, 0, unroll=n <= 16)
    for copy in inputs:
        copy.wait()

    lane = lax.broadcasted_iota(jnp.int32, own_y.shape, 1)
    values = pheno_ref[...].astype(jnp.float32)
    placed = jnp.zeros(own_y.shape, jnp.float32)
    for i in range(s_dev):
        placed = jnp.where(lane == me * s_dev + i, values[:, i : i + 1], placed)
    own_y[...] = placed.astype(jnp.bfloat16)

    panels = dosage_ref.shape[1] // PANEL
    pair_me, samp_me = lax.axis_index("pair"), lax.axis_index("samp")
    pair_n = n // samp
    small = panels <= 16
    if small:
        whole = dosage_ref[...].astype(jnp.float32)

    def fill(i):
        b = partner(pair_me, pair_n - 1 - i, pair_n)
        first = jnp.full((s_dev, LANES), pairs_ref[0, b], jnp.int32)
        second = jnp.full((s_dev, LANES), pairs_ref[1, b], jnp.int32)
        tiles = PANEL // LANES

        def pick(p, kept):
            if small:
                found = [whole[:, p * PANEL + t * LANES :][:, :LANES] for t in range(tiles)]
            else:
                panel = dosage_ref[:, pl.ds(pl.multiple_of(p * PANEL, PANEL), PANEL)]
                found = [
                    panel[:, t * LANES : (t + 1) * LANES].astype(jnp.float32) for t in range(tiles)
                ]
            in_a, in_b = first == p, second == p
            return (
                tuple(jnp.where(in_a, x, old) for x, old in zip(found, kept[0])),
                tuple(jnp.where(in_b, x, old) for x, old in zip(found, kept[1])),
            )

        kept = ((jnp.zeros((s_dev, LANES), jnp.float32),) * tiles,) * 2
        if small:
            for p in range(panels):
                kept = pick(p, kept)
        else:
            kept = lax.fori_loop(0, panels, pick, kept)
        geno_a, geno_b = (jnp.concatenate(x, axis=1).astype(jnp.bfloat16) for x in kept)
        for c in range(samp):
            send_buf[b * samp + c, :, :PANEL] = geno_a
            send_buf[b * samp + c, :, PANEL : PANEL + half] = geno_b[:, c * half : (c + 1) * half]

    far = far_sems.shape[0]
    cells = pl.ds(PANEL, half)

    def reach(b, c, src, dst, sems):
        pltpu.make_async_remote_copy(
            src_ref=src,
            dst_ref=dst,
            send_sem=sems[0],
            recv_sem=sems[1],
            device_id={"pair": b, "samp": c},
            device_id_type=pl.DeviceIdType.MESH,
        ).start()

    def send(b, c, sem=None):
        reach(b, c, send_buf.at[b * samp + c], out_ref.at[me], (send_sem, recv_sem if sem is None else sem))
        reach(b, c, own_y, y_ref.at[me], (y_send, y_recv))

    def send_far(i, b):
        send(b, samp_me, far_sems.at[i])

    def send_rest(i, b):
        for c in range(1, samp):
            other = lax.rem(samp_me + c, samp)
            slab = send_buf.at[b * samp + other]
            reach(b, other, slab.at[:, cells], out_ref.at[me, :, cells], (send_sem, recv_sem))
            reach(b, other, own_y, y_ref.at[me], (y_send, y_recv))

    def pass_on(i, carry):
        back = i + 1 if pair_n & (pair_n - 1) else pair_n - 1 - i
        source = partner(pair_me, back, pair_n) * samp + samp_me
        slab = out_ref.at[source]
        pltpu.make_async_copy(slab, slab, far_sems.at[i]).wait()
        row = out_ref.at[source, :, pl.ds(0, PANEL)]
        for c in range(1, samp):
            reach(pair_me, lax.rem(samp_me + c, samp), row, row, (send_sem, recv_sem))
        return carry

    fill(0)
    pl.semaphore_wait(barrier, n - 1)

    def step(i, carry):
        fill(i + 1)
        b = partner(pair_me, pair_n - 1 - i, pair_n)
        for c in range(samp):
            send(b, c)
        return carry

    def far_step(i, carry):
        fill(i + 1)
        send_far(i, partner(pair_me, pair_n - 1 - i, pair_n))
        return carry

    def rest_step(i, carry):
        send_rest(i, partner(pair_me, pair_n - 1 - i, pair_n))
        return carry

    if small:
        for i in range(far):
            far_step(i, 0)
        for i in range(far):
            rest_step(i, 0)
        for i in range(far, pair_n - 1):
            step(i, 0)
    else:
        lax.fori_loop(0, far, far_step, 0)
        lax.fori_loop(0, far, rest_step, 0)
        lax.fori_loop(far, pair_n - 1, step, 0)
    for c in range(1, samp):
        send(pair_me, lax.rem(samp_me + c, samp))
    pltpu.make_async_copy(send_buf.at[me], out_ref.at[me], recv_sem).start()
    pltpu.make_async_copy(own_y, y_ref.at[me], y_recv).start()

    count = hot_ref.shape[1]
    sample = lax.broadcasted_iota(jnp.int32, (count, 2 * count), 0)
    for r in range(perms_ref.shape[0]):
        order = perms_ref[r : r + 1, :]
        order = jnp.concatenate([order, order], axis=1)
        hot_ref[r] = jnp.where(sample == order, 1.0, 0.0).astype(jnp.bfloat16)

    lax.fori_loop(0, far, pass_on, 0)
    landed = out_ref.at[pl.ds(0, n - far)]
    pltpu.make_async_copy(landed, landed, recv_sem).wait()
    pltpu.make_async_copy(y_ref, y_ref, y_recv).wait()
    for buf, sem in ((send_buf, send_sem), (y_ref, y_send)):
        rest = buf.at[pl.ds(0, n - 1)]
        pltpu.make_async_copy(rest, rest, sem).wait()


def statistics(half, recv_ref, y_ref, hot_ref, out_ref, tiles, sems):
    n, s_dev, _ = recv_ref.shape
    count = n * s_dev
    perms_n = hot_ref.shape[0]
    genes = tiles.shape[0] // perms_n
    rows = jnp.concatenate([recv_ref[i].astype(jnp.float32) for i in range(n)], axis=0)
    geno_a = rows[:, :PANEL]
    geno_b = rows[:, PANEL : PANEL + half]
    pheno = jnp.sum(y_ref[...].astype(jnp.float32), axis=0)[:, :count]
    pheno = jnp.concatenate([pheno] * (8 // genes), axis=0).astype(jnp.bfloat16)

    a_twice = jnp.concatenate([geno_a, geno_a], axis=0).T
    a_low = a_twice.astype(jnp.bfloat16)

    marg_b = jnp.sum(geno_b, axis=0, keepdims=True)
    centred = (geno_b - marg_b * (1.0 / count)) * (1.0 / count**0.5)
    high = centred.astype(jnp.bfloat16)
    low = (centred - high.astype(jnp.float32)).astype(jnp.bfloat16)
    b_split = jnp.concatenate([high, low], axis=0)

    picked = [
        jnp.dot(pheno, hot_ref[r], preferred_element_type=jnp.float32) for r in range(perms_n)
    ]
    slopes = [
        jnp.dot(picked[r].astype(jnp.bfloat16), b_split, preferred_element_type=jnp.float32)
        * (-1.0 / count)
        for r in range(perms_n)
    ]
    copies = []
    for k in range(genes * perms_n):
        g, r = k // perms_n, k % perms_n
        y = picked[r][g : g + 1, :]
        scaled = (a_twice * y).astype(jnp.bfloat16)
        slope = slopes[r][g : g + 1, :]
        slope_high = slope.astype(jnp.bfloat16).astype(jnp.float32)
        slope_low = slope - slope_high
        slope_rows = jnp.concatenate(
            [
                jnp.broadcast_to(slope_high, (count, half)),
                jnp.broadcast_to(slope_low, (count, half)),
            ],
            axis=0,
        ).astype(jnp.bfloat16)
        left = jnp.concatenate([scaled, a_low], axis=1)
        right = jnp.concatenate([b_split, slope_rows], axis=0)
        for part in range(CHUNKS):
            at = pl.ds(part * PANEL // CHUNKS, PANEL // CHUNKS)
            block = left[part * PANEL // CHUNKS : (part + 1) * PANEL // CHUNKS]
            value = jnp.dot(block, right, preferred_element_type=jnp.float32)
            tiles[k, at] = value.astype(jnp.bfloat16)
            copy = pltpu.make_async_copy(
                tiles.at[k, at], out_ref.at[0, k, at], sems.at[k * CHUNKS + part]
            )
            copy.start()
            copies.append(copy)
    for copy in copies:
        copy.wait()


def on_device(dosage, phenotype, perms, pairs):
    samp = lax.axis_size("samp")
    n = lax.axis_size("pair") * samp
    half = PANEL // samp
    s_dev = dosage.shape[0]
    count = n * s_dev
    width = PANEL + half
    y_shape = (phenotype.shape[0], pl.cdiv(n * s_dev, LANES) * LANES)
    kinds = phenotype.shape[0] * perms.shape[0]
    vmem = pl.BlockSpec(memory_space=pltpu.VMEM)
    hbm = pl.BlockSpec(memory_space=pltpu.HBM)
    kept_bytes = 4 * n * s_dev * width + 2 * dosage.size + 16 * count * count + (2 << 20)
    work_bytes = 64 * n * s_dev * PANEL + 4 * kinds * PANEL * half + (8 << 20)
    received = pl.pallas_call(
        functools.partial(exchange, n, samp),
        out_shape=[
            jax.ShapeDtypeStruct((n, s_dev, width), jnp.bfloat16),
            jax.ShapeDtypeStruct((n, *y_shape), jnp.bfloat16),
            jax.ShapeDtypeStruct((perms.shape[0], count, 2 * count), jnp.bfloat16),
        ],
        in_specs=[hbm] * 4,
        out_specs=[pl.BlockSpec(memory_space=pl.ANY)] * 2 + [vmem],
        scratch_shapes=[
            pltpu.SMEM((2, pairs.shape[0]), jnp.int32),
            pltpu.VMEM(perms.shape, jnp.int32),
            pltpu.VMEM(dosage.shape, dosage.dtype),
            pltpu.VMEM(phenotype.shape, phenotype.dtype),
            pltpu.VMEM((n, s_dev, width), jnp.bfloat16),
            pltpu.VMEM(y_shape, jnp.bfloat16),
            pltpu.SemaphoreType.DMA((4,)),
            pltpu.SemaphoreType.DMA,
            pltpu.SemaphoreType.DMA,
            pltpu.SemaphoreType.DMA,
            pltpu.SemaphoreType.DMA,
            pltpu.SemaphoreType.DMA((max(1, n // samp // 4),)),
        ],
        compiler_params=pltpu.CompilerParams(
            collective_id=0, has_side_effects=True, vmem_limit_bytes=min(kept_bytes, 60 << 20)
        ),
        name="exchange",
    )(*(pltpu.with_memory_space_constraint(x, pltpu.HBM) for x in (pairs.T, dosage, phenotype, perms)))
    return pl.pallas_call(
        functools.partial(statistics, half),
        out_shape=jax.ShapeDtypeStruct((1, kinds, PANEL, half), jnp.bfloat16),
        in_specs=[vmem] * 3,
        out_specs=pl.BlockSpec(memory_space=pl.ANY),
        scratch_shapes=[
            pltpu.VMEM((kinds, PANEL, half), jnp.bfloat16),
            pltpu.SemaphoreType.DMA((kinds * CHUNKS,)),
        ],
        compiler_params=pltpu.CompilerParams(vmem_limit_bytes=min(work_bytes, 60 << 20)),
        name="statistics",
    )(*received)


def solution(mesh):
    placed = (P(("rep", "pair", "samp"), None), P(None, ("rep", "pair", "samp")), P(), P())
    return jax.shard_map(
        on_device,
        mesh=mesh,
        in_specs=placed,
        out_specs=P(("rep", "pair"), None, None, "samp"),
        check_vma=False,
    )
```
